32 devices in a mesh: mem: 4 (over y, x), lat: 8 (over z, core).
Axes of the slice: x: 2, y: 2, z: 4, core: 2. Of those that a mesh axis runs over, the one named last changes fastest.
Arguments:
- gradient: float32 [2, 4, 192, 256], P(None, 'mem', 'lat'), may hold values from -24 to 24
- perturbations: bfloat16 [16, 2, 4, 192, 256], P('mem', None, None, 'lat'), may hold values from -6 to 6
- weights: float32 [16, 4, 192, 256], P('mem', None, 'lat'), may hold values from -6 to 6
- lon_taps: float32 [25], replicated, may hold values from 0.05 to 0.3
- lat_taps: float32 [25], replicated, may hold values from 0.05 to 0.3
- lev_taps: float32 [5], replicated, may hold values from 0.2 to 0.7
- level_order: int32 [4], replicated, may hold values from 0 to 3, each once
Outputs:
- updated_weights: float32 [16, 4, 192, 256], P('mem', None, 'lat')
- increment: float32 [2, 4, 192, 256], P(None, 'mem', 'lat')
The draws below stay inside these ranges and needn't reach their ends.
Inputs may be any that keep to these rules, and one draw needn't show every extreme that they name: `level_order`: each level appears in exactly one slot.
All inputs are finite; a program needn't handle non-finite values.
Results may differ from the reference program's by a relative error of at most 0.0003.
Values sent between devices are 32-bit elements; how exact they have to be, the bound alone decides.
A program may use at most 128 MiB of HBM per device.

```python
import math
import jax
import jax.numpy as jnp
from jax import lax

NLON = 256
MEMBERS = 16
NLEV = 4
NLAT = 192
TAPS = 25
LEV_TAPS = 5


def block_levels(stream_key, dims, pieces, low, top_value):
    level = 1.0
    for dim, shards_of in pieces:
        draws = jax.random.uniform(jax.random.fold_in(jax.random.fold_in(stream_key, 6), dim), (shards_of,), jnp.float32, low / len(pieces), top_value / len(pieces))
        level = level * jnp.repeat(jnp.exp(draws), dims[dim] // shards_of).reshape((-1,) + (1,) * (len(dims) - 1 - dim))
    return level


def noise(key, shape, scale, most, cuts=(), kind=jnp.bfloat16):
    entries = scale * jax.random.normal(key, shape, jnp.float32)
    if cuts:
        entries = entries * block_levels(key, shape, cuts, -0.22, 0.18)
    return jnp.clip(entries, -most, most).astype(kind)


def setup_inputs(seed: int = 0) -> dict:
    arg_keys = jax.random.split(jax.random.key(seed), 8)
    return {
        "gradient": noise(arg_keys[0], (2, NLEV, NLAT, NLON), 4.0, 24.0, ((1, 4), (2, 8)), jnp.float32),
        "perturbations": noise(arg_keys[1], (MEMBERS, 2, NLEV, NLAT, NLON), 1.0, 6.0, ((0, 4), (3, 8))),
        "weights": noise(arg_keys[2], (MEMBERS, NLEV, NLAT, NLON), 1.0, 6.0, ((0, 4), (2, 8)), jnp.float32),
        "lon_taps": jnp.clip(jax.random.uniform(arg_keys[3], (TAPS,), jnp.float32, 0.05, 0.3), 0.05, 0.3),
        "lat_taps": jnp.clip(jax.random.uniform(arg_keys[4], (TAPS,), jnp.float32, 0.05, 0.3), 0.05, 0.3),
        "lev_taps": jnp.clip(jax.random.uniform(arg_keys[5], (LEV_TAPS,), jnp.float32, 0.2, 0.7), 0.2, 0.7),
        "level_order": jax.random.permutation(arg_keys[6], NLEV).astype(jnp.int32),
    }


STEP_RATE = 0.5

def lon_forward(values, tap_weights):
    radius = tap_weights.shape[0] // 2
    result = jnp.zeros_like(values)
    for position in range(tap_weights.shape[0]):
        result = result + tap_weights[position] * jnp.roll(values, radius - position, axis=-1)
    return result

def lon_adjoint(values, tap_weights):
    radius = tap_weights.shape[0] // 2
    result = jnp.zeros_like(values)
    for position in range(tap_weights.shape[0]):
        result = result + tap_weights[position] * jnp.roll(values, position - radius, axis=-1)
    return result

def lat_forward(extended, tap_weights):
    width = tap_weights.shape[0]
    out_rows = extended.shape[-2] - width + 1
    result = tap_weights[0] * lax.slice_in_dim(extended, 0, out_rows, axis=extended.ndim - 2)
    for position in range(1, width):
        result = result + tap_weights[position] * lax.slice_in_dim(extended, position, position + out_rows, axis=extended.ndim - 2)
    return result

def lat_adjoint(extended, tap_weights):
    width = tap_weights.shape[0]
    out_rows = extended.shape[-2] - width + 1
    result = tap_weights[0] * lax.slice_in_dim(extended, width - 1, width - 1 + out_rows, axis=extended.ndim - 2)
    for position in range(1, width):
        start_row = width - 1 - position
        result = result + tap_weights[position] * lax.slice_in_dim(extended, start_row, start_row + out_rows, axis=extended.ndim - 2)
    return result

def pad_axis(values, amount, axis_back):
    widths = [(0, 0)] * values.ndim
    widths[values.ndim - axis_back] = (amount, amount)
    return jnp.pad(values, widths)

def lev_forward(values, tap_weights):
    radius = tap_weights.shape[0] // 2
    return lat_forward_levels(pad_axis(values, radius, 3), tap_weights, False)

def lev_adjoint(values, tap_weights):
    radius = tap_weights.shape[0] // 2
    return lat_forward_levels(pad_axis(values, radius, 3), tap_weights, True)

def lat_forward_levels(padded, tap_weights, flipped):
    width = tap_weights.shape[0]
    levels = padded.shape[-3] - width + 1
    result = jnp.zeros(padded.shape[:-3] + (levels,) + padded.shape[-2:], padded.dtype)
    for position in range(width):
        start_level = width - 1 - position if flipped else position
        result = result + tap_weights[position] * lax.slice_in_dim(padded, start_level, start_level + levels, axis=padded.ndim - 3)
    return result

def reference(gradient, perturbations, weights, lon_taps, lat_taps, lev_taps, level_order):
    radius = lat_taps.shape[0] // 2
    norm_factor = 1.0 / math.sqrt(MEMBERS - 1)
    grad_levels = jnp.zeros_like(gradient).at[:, level_order].set(gradient)

    def member_step(running, member_item):
        member_pert, member_weights = member_item
        member_pert = member_pert.astype(jnp.float32)
        products = norm_factor * (member_pert[0] * grad_levels[0] + member_pert[1] * grad_levels[1])
        adjoint = lev_adjoint(lon_adjoint(lat_adjoint(pad_axis(products, radius, 2), lat_taps), lon_taps), lev_taps)
        grad_total = member_weights + adjoint
        updated = member_weights - STEP_RATE * grad_total / (1.0 + jnp.abs(grad_total))
        grid_field = lev_forward(lon_forward(lat_forward(pad_axis(updated, radius, 2), lat_taps), lon_taps), lev_taps)
        return (running + norm_factor * member_pert * grid_field[None], updated)
    inc_levels, updated_weights = lax.scan(member_step, jnp.zeros(gradient.shape, jnp.float32), (perturbations, weights))
    return (updated_weights, inc_levels[:, level_order])
```

```python
import functools
import math

import jax
import jax.numpy as jnp
from jax import lax
from jax.experimental import pallas as pl
from jax.experimental.pallas import tpu as pltpu
from jax.sharding import PartitionSpec as P

STEP_RATE = 0.5
TILE = 8
F32 = jnp.float32
BF16 = jnp.bfloat16


def partner(me, d, n):
    if n & (n - 1):
        return (me + d) % n
    result = 0
    bit = 1
    while bit < n:
        result = result + ((me // bit + d // bit) % 2) * bit
        bit *= 2
    return result


def split(x):
    high = x.astype(BF16)
    return high, (x - high.astype(F32)).astype(BF16)


def dot(a, b, flip=False):
    dims = (((1,), (1 if flip else 0,)), ((), ()))
    return lax.dot_general(a, b, dims, preferred_element_type=F32)


def block_of(index, size, count):
    result = jnp.zeros_like(index)
    for i in range(1, count):
        result = result + (index >= i * size).astype(jnp.int32)
    return result


def kernel(
    n, bands, norm, radius, lev_width,
    g_hbm, p_hbm, w_hbm, lon_t, lat_t, lev_t, order,
    upd_hbm, inc_hbm,
    g_all, p_ref, w_ref, x_ref, u_ref, snd1, rcv1, snd2, rcv2, inc_ref, rs_ref, out_ref,
    c_hi, c_lo, k1_hi, k1_lo, k2_hi, k2_lo,
    load_sem, store_sem, gs, gr, h1s, h1r, h2s, h2r, rss, rsr,
):
    me = lax.axis_index("mem")
    band = lax.axis_index("lat")
    members, _, levels, rows, lons = p_ref.shape
    own_levels = g_hbm.shape[1]
    width = 2 * radius + 1
    full = radius // TILE * TILE
    rem = radius - full
    halo = levels * radius
    fulls = levels * full
    has_low, has_high = band > 0, band < bands - 1

    load_g = pltpu.make_async_copy(g_hbm, g_all.at[0], load_sem.at[0])
    load_p = pltpu.make_async_copy(p_hbm, p_ref, load_sem.at[1])
    load_w = pltpu.make_async_copy(w_hbm, w_ref, load_sem.at[2])
    load_g.start()
    load_p.start()
    load_w.start()

    barrier = pltpu.get_barrier_semaphore()
    mesh_ids = pl.DeviceIdType.MESH
    for d in range(1, n):
        pl.semaphore_signal(
            barrier, inc=1, device_id=(partner(me, d, n), band), device_id_type=mesh_ids
        )

    @pl.when(has_low)
    def _():
        pl.semaphore_signal(barrier, inc=1, device_id=(me, band - 1), device_id_type=mesh_ids)

    @pl.when(has_high)
    def _():
        pl.semaphore_signal(barrier, inc=1, device_id=(me, band + 1), device_id_type=mesh_ids)

    @pl.when(band == 0)
    def _():
        for k in range(members):
            rcv1[k, 0] = jnp.zeros((halo, lons), F32)
            rcv2[k, 0] = jnp.zeros((halo, lons), F32)

    @pl.when(band == bands - 1)
    def _():
        for k in range(members):
            rcv1[k, 1] = jnp.zeros((halo, lons), F32)
            rcv2[k, 1] = jnp.zeros((halo, lons), F32)

    load_g.wait()
    neighbours = has_low.astype(jnp.int32) + has_high.astype(jnp.int32)
    pl.semaphore_wait(barrier, n - 1 + neighbours)

    gathers = []
    for d in range(1, n):
        gathers.append(
            pltpu.make_async_remote_copy(
                src_ref=g_all.at[0],
                dst_ref=g_all.at[d],
                send_sem=gs.at[d - 1],
                recv_sem=gr.at[d - 1],
                device_id=(partner(me, d, n), band),
                device_id_type=mesh_ids,
            )
        )
        gathers[-1].start()

    def source(d):
        return partner(me, d, n) if not n & (n - 1) else (me + n - d) % n

    level_of = [
        order[source(q // own_levels) * own_levels + q % own_levels] for q in range(levels)
    ]

    step = 4 * TILE

    def lon_rows(i, carry):
        first = pl.multiple_of(i * step, step)
        row = lax.broadcasted_iota(jnp.int32, (step, lons), 0) + first
        col = lax.broadcasted_iota(jnp.int32, (step, lons), 1)
        off = col - row + radius
        off = jnp.where(off < 0, off + lons, off)
        off = jnp.where(off >= lons, off - lons, off)
        value = jnp.zeros((step, lons), F32)
        for j in range(width):
            value = jnp.where(off == j, lon_t[j], value)
        high, low = split(value)
        c_hi[pl.ds(first, step), :] = high
        c_lo[pl.ds(first, step), :] = low
        return carry

    lax.fori_loop(0, lons // step, lon_rows, 0)

    total = levels * rows + 2 * halo
    row = lax.broadcasted_iota(jnp.int32, (rows, total), 0)
    col = lax.broadcasted_iota(jnp.int32, (rows, total), 1)
    in_own = col < levels * rows
    in_high = col >= levels * rows + halo
    edge = col - levels * rows - jnp.where(in_high, halo, 0)
    in_full = edge < fulls
    rest = edge - fulls
    lev_own = block_of(col, rows, levels)
    lev_full = block_of(edge, full, levels)
    lev_rest = block_of(rest, rem, levels)
    lev = jnp.where(in_own, lev_own, jnp.where(in_full, lev_full, lev_rest))
    at_full = edge - lev_full * full
    at_rest = rest - lev_rest * rem
    low_pos = jnp.where(in_full, at_full - full, at_rest - radius)
    high_pos = jnp.where(in_full, at_full + rows, at_rest + rows + full)
    pos = jnp.where(in_own, col - lev_own * rows, jnp.where(in_high, high_pos, low_pos))
    shift = pos - row
    lat_adj = jnp.zeros((rows, total), F32)
    lat_fwd = jnp.zeros((rows, total), F32)
    for j in range(width):
        lat_adj = jnp.where(shift == radius - j, lat_t[j], lat_adj)
        lat_fwd = jnp.where(shift == j - radius, lat_t[j], lat_fwd)
    coef = []
    for l in range(levels):
        coef.append([])
        for q in range(levels):
            tap = l - level_of[q] + lev_width // 2
            inside = (tap >= 0) & (tap < lev_width)
            value = lev_t[jnp.clip(tap, 0, lev_width - 1)]
            coef[l].append(jnp.where(inside, value, 0.0))
    for a in range(levels):
        adj_coef = jnp.zeros((rows, total), F32)
        fwd_coef = jnp.zeros((rows, total), F32)
        for b in range(levels):
            adj_coef = jnp.where(lev == b, coef[a][b], adj_coef)
            fwd_coef = jnp.where(lev == b, coef[b][a], fwd_coef)
        at = slice(a * rows, (a + 1) * rows)
        k1_hi[at], k1_lo[at] = split(lat_adj * adj_coef)
        k2_hi[at], k2_lo[at] = split(lat_fwd * fwd_coef)

    load_p.wait()
    load_w.wait()

    def pert(k, v, q):
        return p_ref[k, v, level_of[q]].astype(F32)

    for q in range(levels):
        d, j = divmod(q, own_levels)
        if d and not j:
            gathers[d - 1].wait_recv()
        g0 = g_all[d, 0, j] * norm
        g1 = g_all[d, 1, j] * norm
        for k in range(members):
            x_ref[k, q * rows:(q + 1) * rows] = pert(k, 0, q) * g0 + pert(k, 1, q) * g1

    def halo_copies(snd, rcv, ss, rs, k):
        def make(side, target):
            return pltpu.make_async_remote_copy(
                src_ref=snd.at[k, side],
                dst_ref=rcv.at[k, side],
                send_sem=ss.at[k, side],
                recv_sem=rs.at[k, side],
                device_id=(me, target),
                device_id_type=mesh_ids,
            )

        return make(0, band + 1), make(1, band - 1)

    def send_halo(src, snd, rcv, ss, rs, k):
        for l in range(levels):
            base = l * rows
            snd[k, 0, l * full:(l + 1) * full] = src[k, base + rows - full:base + rows]
            snd[k, 1, l * full:(l + 1) * full] = src[k, base:base + full]
            at = slice(fulls + l * rem, fulls + (l + 1) * rem)
            snd[k, 0, at] = src[k, base + rows - radius:base + rows - full]
            snd[k, 1, at] = src[k, base + full:base + radius]
        up, down = halo_copies(snd, rcv, ss, rs, k)

        @pl.when(has_high)
        def _():
            up.start()

        @pl.when(has_low)
        def _():
            down.start()

    def wait_halo(snd, rcv, ss, rs, k):
        up, down = halo_copies(snd, rcv, ss, rs, k)

        @pl.when(has_low)
        def _():
            up.wait_recv()

        @pl.when(has_high)
        def _():
            down.wait_recv()

    def wait_sent(snd, rcv, ss, rs, k):
        up, down = halo_copies(snd, rcv, ss, rs, k)

        @pl.when(has_high)
        def _():
            up.wait_send()

        @pl.when(has_low)
        def _():
            down.wait_send()

    def apply(src, rcv, k, k_hi, k_lo, flip):
        x = jnp.concatenate([src[k], rcv[k, 0], rcv[k, 1]], axis=0)
        hi, lo = split(x)
        y = dot(k_hi[...], hi) + (dot(k_lo[...], hi) + dot(k_hi[...], lo))
        hi, lo = split(y)
        return dot(hi, c_hi[...], flip) + (dot(lo, c_hi[...], flip) + dot(hi, c_lo[...], flip))

    phase1 = (snd1, rcv1, h1s, h1r)
    phase2 = (snd2, rcv2, h2s, h2r)
    for k in range(members):
        send_halo(x_ref, *phase1, k)

    stores = []
    for k in range(members):
        wait_halo(*phase1, k)
        adjoint = apply(x_ref, rcv1, k, k1_hi, k1_lo, False)
        weight = w_ref[k]
        grad_total = weight + adjoint
        u_ref[k] = weight - STEP_RATE * grad_total / (1.0 + jnp.abs(grad_total))
        send_halo(u_ref, *phase2, k)
        stores.append(pltpu.make_async_copy(u_ref.at[k], upd_hbm.at[k], store_sem.at[k]))
        stores[-1].start()

    for k in range(members):
        wait_halo(*phase2, k)
        field = apply(u_ref, rcv2, k, k2_hi, k2_lo, True)
        for q in range(levels):
            d, j = divmod(q, own_levels)
            part = field[q * rows:(q + 1) * rows] * norm
            for v in range(2):
                term = pert(k, v, q) * part
                inc_ref[d, v, j] = term if k == 0 else inc_ref[d, v, j] + term

    scatters = []
    for d in range(n - 1, 0, -1):
        scatters.append(
            pltpu.make_async_remote_copy(
                src_ref=inc_ref.at[d],
                dst_ref=rs_ref.at[d - 1],
                send_sem=rss.at[d - 1],
                recv_sem=rsr.at[d - 1],
                device_id=(source(d), band),
                device_id_type=mesh_ids,
            )
        )
        scatters[-1].start()
    for copy in stores:
        copy.wait()
    for k in range(members):
        wait_sent(*phase1, k)
        wait_sent(*phase2, k)
    for copy in gathers:
        copy.wait_send()
    for copy in scatters:
        copy.wait_recv()
    result = inc_ref[0]
    for d in range(1, n):
        result = result + rs_ref[d - 1]
    out_ref[...] = result
    store = pltpu.make_async_copy(out_ref, inc_hbm, load_sem.at[0])
    store.start()
    for copy in scatters:
        copy.wait_send()
    store.wait()


def on_device(gradient, perturbations, weights, lon_taps, lat_taps, lev_taps, level_order):
    n, bands = lax.axis_size("mem"), lax.axis_size("lat")
    members, levels, rows, lons = weights.shape
    radius = lat_taps.shape[0] // 2
    norm = 1.0 / math.sqrt(members * n - 1)
    halo = levels * radius
    total = levels * rows + 2 * halo
    vmem, dma = pltpu.VMEM, pltpu.SemaphoreType.DMA
    anywhere = pl.BlockSpec(memory_space=pl.ANY)
    smem = pl.BlockSpec(memory_space=pltpu.SMEM)
    updated, increment = pl.pallas_call(
        functools.partial(kernel, n, bands, norm, radius, lev_taps.shape[0]),
        out_shape=(
            jax.ShapeDtypeStruct((members, levels * rows, lons), F32),
            jax.ShapeDtypeStruct(gradient.shape, F32),
        ),
        in_specs=[anywhere] * 3 + [smem] * 4,
        out_specs=(anywhere, anywhere),
        scratch_shapes=[
            vmem((n,) + gradient.shape, F32),
            vmem(perturbations.shape, BF16),
            vmem((members, levels * rows, lons), F32),
            vmem((members, levels * rows, lons), F32),
            vmem((members, levels * rows, lons), F32),
            vmem((members, 2, halo, lons), F32),
            vmem((members, 2, halo, lons), F32),
            vmem((members, 2, halo, lons), F32),
            vmem((members, 2, halo, lons), F32),
            vmem((n,) + gradient.shape, F32),
            vmem((n - 1,) + gradient.shape, F32),
            vmem(gradient.shape, F32),
            vmem((lons, lons), BF16),
            vmem((lons, lons), BF16),
            vmem((levels * rows, total), BF16),
            vmem((levels * rows, total), BF16),
            vmem((levels * rows, total), BF16),
            vmem((levels * rows, total), BF16),
            dma((3,)),
            dma((members,)),
            dma((n - 1,)),
            dma((n - 1,)),
            dma((members, 2)),
            dma((members, 2)),
            dma((members, 2)),
            dma((members, 2)),
            dma((n - 1,)),
            dma((n - 1,)),
        ],
        compiler_params=pltpu.CompilerParams(collective_id=0, has_side_effects=True),
        name="step",
    )(
        gradient,
        perturbations,
        weights.reshape(members, levels * rows, lons),
        lon_taps,
        lat_taps,
        lev_taps,
        level_order,
    )
    return updated.reshape(weights.shape), increment


def solution(mesh):
    in_specs = (
        P(None, "mem", "lat", None),
        P("mem", None, None, "lat", None),
        P("mem", None, "lat", None),
        P(),
        P(),
        P(),
        P(),
    )
    out_specs = (P("mem", None, "lat", None), P(None, "mem", "lat", None))
    return jax.shard_map(
        on_device, mesh=mesh, in_specs=in_specs, out_specs=out_specs, check_vma=False
    )
```

```python
import functools
import math

import jax
import jax.numpy as jnp
from jax import lax
from jax.experimental import pallas as pl
from jax.experimental.pallas import tpu as pltpu
from jax.sharding import PartitionSpec as P

STEP_RATE = 0.5
TILE = 8
F32 = jnp.float32
BF16 = jnp.bfloat16


def partner(me, d, n):
    if n & (n - 1):
        return (me + d) % n
    result = 0
    bit = 1
    while bit < n:
        result = result + ((me // bit + d // bit) % 2) * bit
        bit *= 2
    return result


def split(x):
    high = x.astype(BF16)
    return high, (x - high.astype(F32)).astype(BF16)


def dot(a, b, flip=False):
    dims = (((1,), (1 if flip else 0,)), ((), ()))
    return lax.dot_general(a, b, dims, preferred_element_type=F32)


def block_of(index, size, count):
    result = jnp.zeros_like(index)
    for i in range(1, count):
        result = result + (index >= i * size).astype(jnp.int32)
    return result


def kernel(
    n, bands, norm, radius, lev_width,
    g_hbm, p_hbm, w_hbm, lon_t, lat_t, lev_t, order,
    u_ref, out_ref,
    g_all, p_ref, w_ref, x_ref, snd1, rcv1, snd2, rcv2, inc_ref, rs_ref,
    c_hi, c_lo, k1_hi, k1_lo, k2_hi, k2_lo,
    load_sem, gs, gr, h1s, h1r, h2s, h2r, rss, rsr,
):
    me = lax.axis_index("mem")
    band = lax.axis_index("lat")
    members, _, levels, rows, lons = p_ref.shape
    own_levels = g_hbm.shape[1]
    width = 2 * radius + 1
    full = radius // TILE * TILE
    rem = radius - full
    halo = levels * radius
    fulls = levels * full
    has_low, has_high = band > 0, band < bands - 1

    load_g = pltpu.make_async_copy(g_hbm, g_all.at[0], load_sem.at[0])
    load_p = pltpu.make_async_copy(p_hbm, p_ref, load_sem.at[1])
    load_w = pltpu.make_async_copy(w_hbm, w_ref, load_sem.at[2])
    load_g.start()
    load_p.start()
    load_w.start()

    barrier = pltpu.get_barrier_semaphore()
    mesh_ids = pl.DeviceIdType.MESH
    for d in range(1, n):
        pl.semaphore_signal(
            barrier, inc=1, device_id=(partner(me, d, n), band), device_id_type=mesh_ids
        )

    @pl.when(has_low)
    def _():
        pl.semaphore_signal(barrier, inc=1, device_id=(me, band - 1), device_id_type=mesh_ids)

    @pl.when(has_high)
    def _():
        pl.semaphore_signal(barrier, inc=1, device_id=(me, band + 1), device_id_type=mesh_ids)

    @pl.when(band == 0)
    def _():
        for k in range(members):
            rcv1[k, 0] = jnp.zeros((halo, lons), F32)
            rcv2[k, 0] = jnp.zeros((halo, lons), F32)

    @pl.when(band == bands - 1)
    def _():
        for k in range(members):
            rcv1[k, 1] = jnp.zeros((halo, lons), F32)
            rcv2[k, 1] = jnp.zeros((halo, lons), F32)

    load_g.wait()
    neighbours = has_low.astype(jnp.int32) + has_high.astype(jnp.int32)
    pl.semaphore_wait(barrier, n - 1 + neighbours)

    gathers = []
    for d in range(1, n):
        gathers.append(
            pltpu.make_async_remote_copy(
                src_ref=g_all.at[0],
                dst_ref=g_all.at[d],
                send_sem=gs.at[d - 1],
                recv_sem=gr.at[d - 1],
                device_id=(partner(me, d, n), band),
                device_id_type=mesh_ids,
            )
        )
        gathers[-1].start()

    def source(d):
        return partner(me, d, n) if not n & (n - 1) else (me + n - d) % n

    level_of = [
        order[source(q // own_levels) * own_levels + q % own_levels] for q in range(levels)
    ]

    step = 4 * TILE

    def lon_rows(i, carry):
        first = pl.multiple_of(i * step, step)
        row = lax.broadcasted_iota(jnp.int32, (step, lons), 0) + first
        col = lax.broadcasted_iota(jnp.int32, (step, lons), 1)
        off = col - row + radius
        off = jnp.where(off < 0, off + lons, off)
        off = jnp.where(off >= lons, off - lons, off)
        value = jnp.zeros((step, lons), F32)
        for j in range(width):
            value = jnp.where(off == j, lon_t[j], value)
        high, low = split(value)
        c_hi[pl.ds(first, step), :] = high
        c_lo[pl.ds(first, step), :] = low
        return carry

    lax.fori_loop(0, lons // step, lon_rows, 0)

    total = levels * rows + 2 * halo
    row = lax.broadcasted_iota(jnp.int32, (rows, total), 0)
    col = lax.broadcasted_iota(jnp.int32, (rows, total), 1)
    in_own = col < levels * rows
    in_high = col >= levels * rows + halo
    edge = col - levels * rows - jnp.where(in_high, halo, 0)
    in_full = edge < fulls
    rest = edge - fulls
    lev_own = block_of(col, rows, levels)
    lev_full = block_of(edge, full, levels)
    lev_rest = block_of(rest, rem, levels)
    lev = jnp.where(in_own, lev_own, jnp.where(in_full, lev_full, lev_rest))
    at_full = edge - lev_full * full
    at_rest = rest - lev_rest * rem
    low_pos = jnp.where(in_full, at_full - full, at_rest - radius)
    high_pos = jnp.where(in_full, at_full + rows, at_rest + rows + full)
    pos = jnp.where(in_own, col - lev_own * rows, jnp.where(in_high, high_pos, low_pos))
    shift = pos - row
    lat_adj = jnp.zeros((rows, total), F32)
    lat_fwd = jnp.zeros((rows, total), F32)
    for j in range(width):
        lat_adj = jnp.where(shift == radius - j, lat_t[j], lat_adj)
        lat_fwd = jnp.where(shift == j - radius, lat_t[j], lat_fwd)
    coef = []
    for l in range(levels):
        coef.append([])
        for q in range(levels):
            tap = l - level_of[q] + lev_width // 2
            inside = (tap >= 0) & (tap < lev_width)
            value = lev_t[jnp.clip(tap, 0, lev_width - 1)]
            coef[l].append(jnp.where(inside, value, 0.0))
    for a in range(levels):
        adj_coef = jnp.zeros((rows, total), F32)
        fwd_coef = jnp.zeros((rows, total), F32)
        for b in range(levels):
            adj_coef = jnp.where(lev == b, coef[a][b], adj_coef)
            fwd_coef = jnp.where(lev == b, coef[b][a], fwd_coef)
        at = slice(a * rows, (a + 1) * rows)
        k1_hi[at], k1_lo[at] = split(lat_adj * adj_coef)
        k2_hi[at], k2_lo[at] = split(lat_fwd * fwd_coef)

    load_p.wait()
    load_w.wait()

    def pert(k, v, q):
        return p_ref[k, v, level_of[q]].astype(F32)

    for q in range(levels):
        d, j = divmod(q, own_levels)
        if d and not j:
            gathers[d - 1].wait_recv()
        g0 = g_all[d, 0, j] * norm
        g1 = g_all[d, 1, j] * norm
        for k in range(members):
            x_ref[k, q * rows:(q + 1) * rows] = pert(k, 0, q) * g0 + pert(k, 1, q) * g1

    def halo_copies(snd, rcv, ss, rs, k):
        def make(side, target):
            return pltpu.make_async_remote_copy(
                src_ref=snd.at[k, side],
                dst_ref=rcv.at[k, side],
                send_sem=ss.at[k, side],
                recv_sem=rs.at[k, side],
                device_id=(me, target),
                device_id_type=mesh_ids,
            )

        return make(0, band + 1), make(1, band - 1)

    def send_halo(src, snd, rcv, ss, rs, k):
        for l in range(levels):
            base = l * rows
            snd[k, 0, l * full:(l + 1) * full] = src[k, base + rows - full:base + rows]
            snd[k, 1, l * full:(l + 1) * full] = src[k, base:base + full]
            at = slice(fulls + l * rem, fulls + (l + 1) * rem)
            snd[k, 0, at] = src[k, base + rows - radius:base + rows - full]
            snd[k, 1, at] = src[k, base + full:base + radius]
        up, down = halo_copies(snd, rcv, ss, rs, k)

        @pl.when(has_high)
        def _():
            up.start()

        @pl.when(has_low)
        def _():
            down.start()

    def wait_halo(snd, rcv, ss, rs, k):
        up, down = halo_copies(snd, rcv, ss, rs, k)

        @pl.when(has_low)
        def _():
            up.wait_recv()

        @pl.when(has_high)
        def _():
            down.wait_recv()

    def wait_sent(snd, rcv, ss, rs, k):
        up, down = halo_copies(snd, rcv, ss, rs, k)

        @pl.when(has_high)
        def _():
            up.wait_send()

        @pl.when(has_low)
        def _():
            down.wait_send()

    def apply(src, rcv, k, k_hi, k_lo, flip):
        x = jnp.concatenate([src[k], rcv[k, 0], rcv[k, 1]], axis=0)
        hi, lo = split(x)
        y = dot(k_hi[...], hi) + (dot(k_lo[...], hi) + dot(k_hi[...], lo))
        hi, lo = split(y)
        return dot(hi, c_hi[...], flip) + (dot(lo, c_hi[...], flip) + dot(hi, c_lo[...], flip))

    phase1 = (snd1, rcv1, h1s, h1r)
    phase2 = (snd2, rcv2, h2s, h2r)
    for k in range(members):
        send_halo(x_ref, *phase1, k)

    for k in range(members):
        wait_halo(*phase1, k)
        adjoint = apply(x_ref, rcv1, k, k1_hi, k1_lo, False)
        weight = w_ref[k]
        grad_total = weight + adjoint
        u_ref[k] = weight - STEP_RATE * grad_total / (1.0 + jnp.abs(grad_total))
        send_halo(u_ref, *phase2, k)

    for k in range(members):
        wait_halo(*phase2, k)
        field = apply(u_ref, rcv2, k, k2_hi, k2_lo, True)
        for q in range(levels):
            d, j = divmod(q, own_levels)
            part = field[q * rows:(q + 1) * rows] * norm
            for v in range(2):
                term = pert(k, v, q) * part
                inc_ref[d, v, j] = term if k == 0 else inc_ref[d, v, j] + term

    scatters = []
    for d in range(n - 1, 0, -1):
        scatters.append(
            pltpu.make_async_remote_copy(
                src_ref=inc_ref.at[d],
                dst_ref=rs_ref.at[d - 1],
                send_sem=rss.at[d - 1],
                recv_sem=rsr.at[d - 1],
                device_id=(source(d), band),
                device_id_type=mesh_ids,
            )
        )
        scatters[-1].start()
    for k in range(members):
        wait_sent(*phase1, k)
        wait_sent(*phase2, k)
    for copy in gathers:
        copy.wait_send()
    for copy in scatters:
        copy.wait_recv()
    result = inc_ref[0]
    for d in range(1, n):
        result = result + rs_ref[d - 1]
    out_ref[...] = result
    for copy in scatters:
        copy.wait_send()


def on_device(gradient, perturbations, weights, lon_taps, lat_taps, lev_taps, level_order):
    n, bands = lax.axis_size("mem"), lax.axis_size("lat")
    members, levels, rows, lons = weights.shape
    radius = lat_taps.shape[0] // 2
    norm = 1.0 / math.sqrt(members * n - 1)
    halo = levels * radius
    total = levels * rows + 2 * halo
    vmem, dma = pltpu.VMEM, pltpu.SemaphoreType.DMA
    anywhere = pl.BlockSpec(memory_space=pl.ANY)
    in_vmem = pl.BlockSpec(memory_space=pltpu.VMEM)
    smem = pl.BlockSpec(memory_space=pltpu.SMEM)
    updated, increment = pl.pallas_call(
        functools.partial(kernel, n, bands, norm, radius, lev_taps.shape[0]),
        out_shape=(
            vmem((members, levels * rows, lons), F32),
            vmem(gradient.shape, F32),
        ),
        in_specs=[anywhere] * 3 + [smem] * 4,
        out_specs=(in_vmem, in_vmem),
        scratch_shapes=[
            vmem((n,) + gradient.shape, F32),
            vmem(perturbations.shape, BF16),
            vmem((members, levels * rows, lons), F32),
            vmem((members, levels * rows, lons), F32),
            vmem((members, 2, halo, lons), F32),
            vmem((members, 2, halo, lons), F32),
            vmem((members, 2, halo, lons), F32),
            vmem((members, 2, halo, lons), F32),
            vmem((n,) + gradient.shape, F32),
            vmem((n - 1,) + gradient.shape, F32),
            vmem((lons, lons), BF16),
            vmem((lons, lons), BF16),
            vmem((levels * rows, total), BF16),
            vmem((levels * rows, total), BF16),
            vmem((levels * rows, total), BF16),
            vmem((levels * rows, total), BF16),
            dma((3,)),
            dma((n - 1,)),
            dma((n - 1,)),
            dma((members, 2)),
            dma((members, 2)),
            dma((members, 2)),
            dma((members, 2)),
            dma((n - 1,)),
            dma((n - 1,)),
        ],
        compiler_params=pltpu.CompilerParams(collective_id=0, has_side_effects=True),
        name="step",
    )(
        gradient,
        perturbations,
        weights.reshape(members, levels * rows, lons),
        lon_taps,
        lat_taps,
        lev_taps,
        level_order,
    )
    return updated.reshape(weights.shape), increment


def solution(mesh):
    in_specs = (
        P(None, "mem", "lat", None),
        P("mem", None, None, "lat", None),
        P("mem", None, "lat", None),
        P(),
        P(),
        P(),
        P(),
    )
    out_specs = (P("mem", None, "lat", None), P(None, "mem", "lat", None))
    return jax.shard_map(
        on_device, mesh=mesh, in_specs=in_specs, out_specs=out_specs, check_vma=False
    )
```

```python
import functools
import math

import jax
import jax.numpy as jnp
from jax import lax
from jax.experimental import pallas as pl
from jax.experimental.pallas import tpu as pltpu
from jax.sharding import PartitionSpec as P

STEP_RATE = 0.5
TILE = 8
F32 = jnp.float32
BF16 = jnp.bfloat16


def partner(me, d, n):
    if n & (n - 1):
        return (me + d) % n
    result = 0
    bit = 1
    while bit < n:
        result = result + ((me // bit + d // bit) % 2) * bit
        bit *= 2
    return result


def split(x):
    high = x.astype(BF16)
    return high, (x - high.astype(F32)).astype(BF16)


def dot(a, b, flip=False):
    dims = (((1,), (1 if flip else 0,)), ((), ()))
    return lax.dot_general(a, b, dims, preferred_element_type=F32)


def block_of(index, size, count):
    result = jnp.zeros_like(index)
    for i in range(1, count):
        result = result + (index >= i * size).astype(jnp.int32)
    return result


def kernel(
    n, bands, norm, radius, lev_width,
    g_hbm, p_hbm, w_hbm, lon_t, lat_t, lev_t, order,
    u_ref, out_ref,
    g_all, p_ref, w_ref, x_ref, snd1, rcv1, snd2, rcv2, inc_ref, rs_ref,
    c_hi, c_lo, k1_hi, k1_lo, k2_hi, k2_lo,
    load_sem, known_sem, gs, gr, h1s, h1r, h2s, h2r, rss, rsr,
):
    me = lax.axis_index("mem")
    band = lax.axis_index("lat")
    members, _, levels, rows, lons = p_ref.shape
    own_levels = g_hbm.shape[1]
    width = 2 * radius + 1
    full = radius // TILE * TILE
    rem = radius - full
    halo = levels * radius
    fulls = levels * full
    has_low, has_high = band > 0, band < bands - 1

    load_g = pltpu.make_async_copy(g_hbm, g_all.at[0], load_sem.at[0])
    load_p = pltpu.make_async_copy(p_hbm, p_ref, load_sem.at[1])
    load_w = pltpu.make_async_copy(w_hbm, w_ref, load_sem.at[2])
    load_g.start()
    load_p.start()
    load_w.start()

    barrier = pltpu.get_barrier_semaphore()
    mesh_ids = pl.DeviceIdType.MESH
    cube = not n & (n - 1)
    direct = [d for d in range(1, n) if not cube or not d & (d - 1)]

    def greet(semaphore):
        for d in direct:
            pl.semaphore_signal(
                semaphore, inc=1, device_id=(partner(me, d, n), band), device_id_type=mesh_ids
            )

    greet(barrier)

    @pl.when(has_low)
    def _():
        pl.semaphore_signal(barrier, inc=1, device_id=(me, band - 1), device_id_type=mesh_ids)

    @pl.when(has_high)
    def _():
        pl.semaphore_signal(barrier, inc=1, device_id=(me, band + 1), device_id_type=mesh_ids)

    @pl.when(band == 0)
    def _():
        for k in range(members):
            rcv1[k, 0] = jnp.zeros((halo, lons), F32)
            rcv2[k, 0] = jnp.zeros((halo, lons), F32)

    @pl.when(band == bands - 1)
    def _():
        for k in range(members):
            rcv1[k, 1] = jnp.zeros((halo, lons), F32)
            rcv2[k, 1] = jnp.zeros((halo, lons), F32)

    load_g.wait()
    neighbours = has_low.astype(jnp.int32) + has_high.astype(jnp.int32)
    pl.semaphore_wait(barrier, len(direct) + neighbours)

    gathers = {}
    for hops in range(1, len(direct) + 1 if cube else 2):
        if hops > 1:
            greet(known_sem.at[hops - 2])
            pl.semaphore_wait(known_sem.at[hops - 2], len(direct))
        for d in range(1, n):
            if cube and bin(d).count("1") != hops:
                continue
            gathers[d] = pltpu.make_async_remote_copy(
                src_ref=g_all.at[0],
                dst_ref=g_all.at[d],
                send_sem=gs.at[d - 1],
                recv_sem=gr.at[d - 1],
                device_id=(partner(me, d, n), band),
                device_id_type=mesh_ids,
            )
            gathers[d].start()

    def source(d):
        return partner(me, d, n) if not n & (n - 1) else (me + n - d) % n

    level_of = [
        order[source(q // own_levels) * own_levels + q % own_levels] for q in range(levels)
    ]

    step = 4 * TILE

    def lon_rows(i, carry):
        first = pl.multiple_of(i * step, step)
        row = lax.broadcasted_iota(jnp.int32, (step, lons), 0) + first
        col = lax.broadcasted_iota(jnp.int32, (step, lons), 1)
        off = col - row + radius
        off = jnp.where(off < 0, off + lons, off)
        off = jnp.where(off >= lons, off - lons, off)
        value = jnp.zeros((step, lons), F32)
        for j in range(width):
            value = jnp.where(off == j, lon_t[j], value)
        high, low = split(value)
        c_hi[pl.ds(first, step), :] = high
        c_lo[pl.ds(first, step), :] = low
        return carry

    lax.fori_loop(0, lons // step, lon_rows, 0)

    total = levels * rows + 2 * halo
    row = lax.broadcasted_iota(jnp.int32, (rows, total), 0)
    col = lax.broadcasted_iota(jnp.int32, (rows, total), 1)
    in_own = col < levels * rows
    in_high = col >= levels * rows + halo
    edge = col - levels * rows - jnp.where(in_high, halo, 0)
    in_full = edge < fulls
    rest = edge - fulls
    lev_own = block_of(col, rows, levels)
    lev_full = block_of(edge, full, levels)
    lev_rest = block_of(rest, rem, levels)
    lev = jnp.where(in_own, lev_own, jnp.where(in_full, lev_full, lev_rest))
    at_full = edge - lev_full * full
    at_rest = rest - lev_rest * rem
    low_pos = jnp.where(in_full, at_full - full, at_rest - radius)
    high_pos = jnp.where(in_full, at_full + rows, at_rest + rows + full)
    pos = jnp.where(in_own, col - lev_own * rows, jnp.where(in_high, high_pos, low_pos))
    shift = pos - row
    lat_adj = jnp.zeros((rows, total), F32)
    lat_fwd = jnp.zeros((rows, total), F32)
    for j in range(width):
        lat_adj = jnp.where(shift == radius - j, lat_t[j], lat_adj)
        lat_fwd = jnp.where(shift == j - radius, lat_t[j], lat_fwd)
    coef = []
    for l in range(levels):
        coef.append([])
        for q in range(levels):
            tap = l - level_of[q] + lev_width // 2
            inside = (tap >= 0) & (tap < lev_width)
            value = lev_t[jnp.clip(tap, 0, lev_width - 1)]
            coef[l].append(jnp.where(inside, value, 0.0))
    for a in range(levels):
        adj_coef = jnp.zeros((rows, total), F32)
        fwd_coef = jnp.zeros((rows, total), F32)
        for b in range(levels):
            adj_coef = jnp.where(lev == b, coef[a][b], adj_coef)
            fwd_coef = jnp.where(lev == b, coef[b][a], fwd_coef)
        at = slice(a * rows, (a + 1) * rows)
        k1_hi[at], k1_lo[at] = split(lat_adj * adj_coef)
        k2_hi[at], k2_lo[at] = split(lat_fwd * fwd_coef)

    load_p.wait()
    load_w.wait()

    def pert(k, v, q):
        return p_ref[k, v, level_of[q]].astype(F32)

    for q in range(levels):
        d, j = divmod(q, own_levels)
        if d and not j:
            gathers[d].wait_recv()
        g0 = g_all[d, 0, j] * norm
        g1 = g_all[d, 1, j] * norm
        for k in range(members):
            x_ref[k, q * rows:(q + 1) * rows] = pert(k, 0, q) * g0 + pert(k, 1, q) * g1

    def halo_copies(snd, rcv, ss, rs, k):
        def make(side, target):
            return pltpu.make_async_remote_copy(
                src_ref=snd.at[k, side],
                dst_ref=rcv.at[k, side],
                send_sem=ss.at[k, side],
                recv_sem=rs.at[k, side],
                device_id=(me, target),
                device_id_type=mesh_ids,
            )

        return make(0, band + 1), make(1, band - 1)

    def send_halo(src, snd, rcv, ss, rs, k):
        for l in range(levels):
            base = l * rows
            snd[k, 0, l * full:(l + 1) * full] = src[k, base + rows - full:base + rows]
            snd[k, 1, l * full:(l + 1) * full] = src[k, base:base + full]
            at = slice(fulls + l * rem, fulls + (l + 1) * rem)
            snd[k, 0, at] = src[k, base + rows - radius:base + rows - full]
            snd[k, 1, at] = src[k, base + full:base + radius]
        up, down = halo_copies(snd, rcv, ss, rs, k)

        @pl.when(has_high)
        def _():
            up.start()

        @pl.when(has_low)
        def _():
            down.start()

    def wait_halo(snd, rcv, ss, rs, k):
        up, down = halo_copies(snd, rcv, ss, rs, k)

        @pl.when(has_low)
        def _():
            up.wait_recv()

        @pl.when(has_high)
        def _():
            down.wait_recv()

    def wait_sent(snd, rcv, ss, rs, k):
        up, down = halo_copies(snd, rcv, ss, rs, k)

        @pl.when(has_high)
        def _():
            up.wait_send()

        @pl.when(has_low)
        def _():
            down.wait_send()

    def apply(src, rcv, k, k_hi, k_lo, flip):
        x = jnp.concatenate([src[k], rcv[k, 0], rcv[k, 1]], axis=0)
        hi, lo = split(x)
        y = dot(k_hi[...], hi) + (dot(k_lo[...], hi) + dot(k_hi[...], lo))
        hi, lo = split(y)
        return dot(hi, c_hi[...], flip) + (dot(lo, c_hi[...], flip) + dot(hi, c_lo[...], flip))

    phase1 = (snd1, rcv1, h1s, h1r)
    phase2 = (snd2, rcv2, h2s, h2r)
    for k in range(members):
        send_halo(x_ref, *phase1, k)

    for k in range(members):
        wait_halo(*phase1, k)
        adjoint = apply(x_ref, rcv1, k, k1_hi, k1_lo, False)
        weight = w_ref[k]
        grad_total = weight + adjoint
        u_ref[k] = weight - STEP_RATE * grad_total / (1.0 + jnp.abs(grad_total))
        send_halo(u_ref, *phase2, k)

    scatters = []
    for k in range(members):
        wait_halo(*phase2, k)
        field = apply(u_ref, rcv2, k, k2_hi, k2_lo, True)
        for d in range(n - 1, -1, -1):
            for j in range(own_levels):
                q = d * own_levels + j
                part = field[q * rows:(q + 1) * rows] * norm
                for v in range(2):
                    term = pert(k, v, q) * part
                    inc_ref[d, v, j] = term if k == 0 else inc_ref[d, v, j] + term
            if d and k == members - 1:
                scatters.append(
                    pltpu.make_async_remote_copy(
                        src_ref=inc_ref.at[d],
                        dst_ref=rs_ref.at[d - 1],
                        send_sem=rss.at[d - 1],
                        recv_sem=rsr.at[d - 1],
                        device_id=(source(d), band),
                        device_id_type=mesh_ids,
                    )
                )
                scatters[-1].start()
    for k in range(members):
        wait_sent(*phase1, k)
        wait_sent(*phase2, k)
    for copy in gathers.values():
        copy.wait_send()
    for copy in scatters:
        copy.wait_recv()
    result = inc_ref[0]
    for d in range(1, n):
        result = result + rs_ref[d - 1]
    out_ref[...] = result
    for copy in scatters:
        copy.wait_send()


def write_out(u_ref, inc_ref, upd_hbm, inc_hbm, sem):
    first = pltpu.make_async_copy(u_ref, upd_hbm, sem.at[0])
    second = pltpu.make_async_copy(inc_ref, inc_hbm, sem.at[1])
    first.start()
    second.start()
    first.wait()
    second.wait()


def on_device(gradient, perturbations, weights, lon_taps, lat_taps, lev_taps, level_order):
    n, bands = lax.axis_size("mem"), lax.axis_size("lat")
    members, levels, rows, lons = weights.shape
    radius = lat_taps.shape[0] // 2
    norm = 1.0 / math.sqrt(members * n - 1)
    halo = levels * radius
    total = levels * rows + 2 * halo
    vmem, dma = pltpu.VMEM, pltpu.SemaphoreType.DMA
    anywhere = pl.BlockSpec(memory_space=pl.ANY)
    in_vmem = pl.BlockSpec(memory_space=pltpu.VMEM)
    smem = pl.BlockSpec(memory_space=pltpu.SMEM)
    updated, increment = pl.pallas_call(
        functools.partial(kernel, n, bands, norm, radius, lev_taps.shape[0]),
        out_shape=(
            vmem((members, levels * rows, lons), F32),
            vmem(gradient.shape, F32),
        ),
        in_specs=[anywhere] * 3 + [smem] * 4,
        out_specs=(in_vmem, in_vmem),
        scratch_shapes=[
            vmem((n,) + gradient.shape, F32),
            vmem(perturbations.shape, BF16),
            vmem((members, levels * rows, lons), F32),
            vmem((members, levels * rows, lons), F32),
            vmem((members, 2, halo, lons), F32),
            vmem((members, 2, halo, lons), F32),
            vmem((members, 2, halo, lons), F32),
            vmem((members, 2, halo, lons), F32),
            vmem((n,) + gradient.shape, F32),
            vmem((n - 1,) + gradient.shape, F32),
            vmem((lons, lons), BF16),
            vmem((lons, lons), BF16),
            vmem((levels * rows, total), BF16),
            vmem((levels * rows, total), BF16),
            vmem((levels * rows, total), BF16),
            vmem((levels * rows, total), BF16),
            dma((3,)),
            pltpu.SemaphoreType.REGULAR((max(1, n.bit_length() - 2),)),
            dma((n - 1,)),
            dma((n - 1,)),
            dma((members, 2)),
            dma((members, 2)),
            dma((members, 2)),
            dma((members, 2)),
            dma((n - 1,)),
            dma((n - 1,)),
        ],
        compiler_params=pltpu.CompilerParams(collective_id=0, has_side_effects=True),
        name="step",
    )(
        gradient,
        perturbations,
        weights.reshape(members, levels * rows, lons),
        lon_taps,
        lat_taps,
        lev_taps,
        level_order,
    )
    updated, increment = pl.pallas_call(
        write_out,
        out_shape=(
            jax.ShapeDtypeStruct(updated.shape, F32),
            jax.ShapeDtypeStruct(increment.shape, F32),
        ),
        in_specs=[in_vmem] * 2,
        out_specs=(anywhere, anywhere),
        scratch_shapes=[dma((2,))],
        name="write_out",
    )(
        pltpu.with_memory_space_constraint(updated, pltpu.VMEM),
        pltpu.with_memory_space_constraint(increment, pltpu.VMEM),
    )
    return updated.reshape(weights.shape), increment


def solution(mesh):
    in_specs = (
        P(None, "mem", "lat", None),
        P("mem", None, None, "lat", None),
        P("mem", None, "lat", None),
        P(),
        P(),
        P(),
        P(),
    )
    out_specs = (P("mem", None, "lat", None), P(None, "mem", "lat", None))
    return jax.shard_map(
        on_device, mesh=mesh, in_specs=in_specs, out_specs=out_specs, check_vma=False
    )
```
